256 devices in a mesh: inner: 8 (over x_lo, y), outer: 32 (over z, x_hi, core).
Axes of the slice: x: 4 (x_hi: 2, x_lo: 2; x = x_hi * 2 + x_lo), y: 4, z: 8, core: 2. Of those that a mesh axis runs over, the one named last changes fastest.
Arguments:
- queries: float32 [98304, 8, 128], P(('inner', 'outer')), may hold values from -50 to 50
- key_rows: float32 [98304, 128], P(('inner', 'outer')), may hold values from -50 to 50
- value_rows: float32 [98304, 128], P(('inner', 'outer')), may hold values from -6 to 6
- doc_lengths: int32 [256], replicated, may hold values from 1 to 3072, 98304 in all
Outputs:
- attended: float32 [98304, 8, 128], P(('inner', 'outer'))
The draws below stay inside these ranges and needn't reach their ends.
Inputs may be any that keep to these rules, and one draw needn't show every extreme that they name: `doc_lengths`: each document has at most 3072 tokens, and one has exactly that many.
All inputs are finite; a program needn't handle non-finite values.
Results may differ from the reference program's by a relative error of at most 0.0003.
Values sent between devices are 32-bit elements; how exact they have to be, the bound alone decides.
No kernel may reach another device: no remote copies, remote signals or barrier semaphores. Data moves between devices by JAX's collectives and lax.ppermute only.
A program may use at most 64 MiB of HBM per device.

```python
import math
import jax
import jax.numpy as jnp
import numpy as np
from jax import lax

H = 8
HD = 128
TOK_DEV = 384
REACH = 8
TOKENS = 98304
DOCS = 256


def shared_draw(key):
    base = jax.random.fold_in(key, 11)
    key_raw = jnp.clip(jax.random.normal(jax.random.fold_in(base, 1), (TOKENS, HD), jnp.float32), -6.0, 6.0)
    query_raw = jnp.clip(jax.random.normal(jax.random.fold_in(base, 2), (TOKENS, H, HD), jnp.float32), -6.0, 6.0)
    return (query_raw, key_raw)


def draw_queries(key, part):
    return shared_draw(key)[0]


def draw_key_rows(key, part):
    return shared_draw(key)[1]


def block_scale(key, dims, shards, smallest, top_value):
    loudness = 1.0
    for position, parts in shards:
        heights = jax.random.uniform(jax.random.fold_in(jax.random.fold_in(key, 6), position), (parts,), jnp.float32, smallest / len(shards), top_value / len(shards))
        loudness = loudness * jnp.repeat(jnp.exp(heights), dims[position] // parts).reshape((-1,) + (1,) * (len(dims) - 1 - position))
    return loudness


def profile(amount, total, bound, skew):
    portions = [(1 << 20) // math.isqrt(rank ** skew) + 1 for rank in range(2, amount + 1)]
    rest, given = total - bound - (amount - 1), [1] * (amount - 1)
    while rest > 0:
        candidates = [i for i in range(amount - 1) if given[i] < bound]
        whole, left = sum([portions[i] for i in candidates]), rest
        for i in candidates:
            addition = min(bound - given[i], max(1, left * portions[i] // whole), rest)
            given[i] = given[i] + addition
            rest = rest - addition
    return np.array([bound] + given)


def ragged_sizes(stream_key, count, total, limit, skew):
    if count == 2:
        one = jax.random.randint(stream_key, (), max(1, total - limit), min(limit, total - 1) + 1)
        return jnp.stack([one, total - one])
    lengths = jnp.asarray(profile(count, total, limit, skew), jnp.int32)
    twos = (count - 1) // 2
    source_of, taker = lengths[1:1 + 2 * twos:2], lengths[2:2 + 2 * twos:2]
    slack = jnp.minimum(source_of - 1, limit - taker)
    moved = jax.random.randint(jax.random.fold_in(stream_key, 1), (twos,), 0, 1 << 20) % (slack + 1)
    lengths = lengths.at[1:1 + 2 * twos:2].set(source_of - moved).at[2:2 + 2 * twos:2].set(taker + moved)
    return lengths[jax.random.permutation(jax.random.fold_in(stream_key, 2), count)]


def bell_draw(stream_key, dims, deviation, reach, pieces=(), kind=jnp.bfloat16):
    values = jax.random.normal(stream_key, dims, jnp.float32) * deviation
    if len(pieces) > 0:
        values = block_scale(stream_key, dims, pieces, -0.22, 0.18) * values
    return jnp.clip(values, min=-reach, max=reach).astype(kind)


def setup_inputs(seed: int = 0) -> dict:
    key_list = jax.random.split(jax.random.key(seed), 5)
    queries = draw_queries(jax.random.fold_in(key_list[4], 71), 0)
    key_rows = draw_key_rows(jax.random.fold_in(key_list[4], 71), 0)
    value_rows = bell_draw(key_list[2], (TOKENS, HD), 1.0, 6.0, ((0, 256),), jnp.float32)
    doc_lengths = ragged_sizes(key_list[3], DOCS, TOKENS, REACH * TOK_DEV, 2).astype(jnp.int32)
    return dict(queries=queries, key_rows=key_rows, value_rows=value_rows, doc_lengths=doc_lengths)


def doc_index(positions, starts):
    return jnp.sum((starts[None, :] <= positions[:, None]).astype(jnp.int32), axis=1) - 1


def reference(queries, key_rows, value_rows, doc_lengths):
    starts = jnp.cumsum(doc_lengths) - doc_lengths
    positions = jnp.arange(TOKENS, dtype=jnp.int32)
    docs = doc_index(positions, starts)
    span = REACH * TOK_DEV
    pad_keys = jnp.concatenate([jnp.zeros((span, HD), key_rows.dtype), key_rows], axis=0)
    pad_values = jnp.concatenate([jnp.zeros((span, HD), value_rows.dtype), value_rows], axis=0)
    pad_pos = jnp.concatenate([jnp.arange(span, dtype=jnp.int32) - span, positions])
    pad_docs = jnp.concatenate([jnp.full((span,), -1, jnp.int32), docs])
    factor = 1.0 / (HD ** 0.5)

    def block(index):
        begin = (index * TOK_DEV).astype(jnp.int32)
        q_rows = lax.dynamic_slice_in_dim(queries, begin, TOK_DEV, 0)
        q_pos = lax.dynamic_slice_in_dim(positions, begin, TOK_DEV, 0)
        q_doc = lax.dynamic_slice_in_dim(docs, begin, TOK_DEV, 0)
        k_rows = lax.dynamic_slice_in_dim(pad_keys, begin, span + TOK_DEV, 0)
        v_rows = lax.dynamic_slice_in_dim(pad_values, begin, span + TOK_DEV, 0)
        k_pos = lax.dynamic_slice_in_dim(pad_pos, begin, span + TOK_DEV, 0)
        k_doc = lax.dynamic_slice_in_dim(pad_docs, begin, span + TOK_DEV, 0)
        scores = jnp.einsum("thd,sd->hts", q_rows.astype(jnp.float32), k_rows.astype(jnp.float32), precision=lax.Precision.HIGHEST) * factor
        allowed = (k_pos[None, :] <= q_pos[:, None]) & (k_doc[None, :] == q_doc[:, None])
        peak = jnp.max(jnp.where(allowed[None], scores, -1.0e30), axis=2)
        weights = jnp.where(allowed[None], jnp.exp(scores - peak[:, :, None]), 0.0)
        totals = jnp.sum(weights, axis=2)
        mixed = jnp.einsum("hts,sd->htd", weights, v_rows.astype(jnp.float32), precision=lax.Precision.HIGHEST)
        return jnp.transpose(mixed / totals[:, :, None], (1, 0, 2))

    blocks = lax.map(block, jnp.arange(TOKENS // TOK_DEV, dtype=jnp.int32))
    return blocks.reshape(TOKENS, H, HD)
```

```python
import functools
import math

import jax
import jax.numpy as jnp
from jax import lax
from jax.experimental import pallas as pl
from jax.experimental.pallas import tpu as pltpu
from jax.sharding import PartitionSpec as P

AXES = ("inner", "outer")
REACH = 8
NEGATIVE = -1e30
TILE = 128
CHUNK = 256
BF16 = jnp.bfloat16
F32 = jnp.float32


def halves(x):
    high = x.astype(BF16)
    return high, (x - high.astype(F32)).astype(BF16)


def place(kv_ref, start, k_buf, v_buf):
    rows = kv_ref.shape[0] // 2
    at = pl.ds(pl.multiple_of(start, 128), rows)
    high, low = halves(kv_ref[0:rows, :])
    k_buf[at, 0:128] = high
    k_buf[at, 128:256] = high
    k_buf[at, 256:384] = low
    high, low = halves(kv_ref[rows : 2 * rows, :])
    for turn in range(2):
        at = pl.ds(pl.multiple_of(start + turn * 2 * rows, 128), rows)
        v_buf[at, 0:128] = high
        v_buf[at, 128:256] = low


def step(rows, first, own, base, q_buf, k_buf, v_buf, qs_ref, acc_ref, m_ref, l_ref, row_pos):
    keys = k_buf.shape[0]
    nt = (((1,), (1,)), ((), ()))
    q_all = q_buf[rows, :]
    scores = lax.dot_general(q_all, k_buf[:, 0:256], nt, preferred_element_type=F32)
    scores += lax.dot_general(q_all[:, 0:128], k_buf[:, 256:384], nt, preferred_element_type=F32)
    low = qs_ref[rows, :] - base
    lane = lax.broadcasted_iota(jnp.int32, low.shape, 1)
    parts = []
    for c in range(keys // 128):
        s = scores[:, c * 128 : (c + 1) * 128]
        allowed = lane + c * 128 >= low
        if own:
            allowed &= lane + c * 128 <= row_pos - base
        parts.append(jnp.where(allowed, s, NEGATIVE))
    top = functools.reduce(jnp.maximum, parts)
    top = jnp.broadcast_to(jnp.max(top, axis=1, keepdims=True), top.shape)
    if not first:
        before = m_ref[rows, :]
        top = jnp.maximum(before, top)
        shrink = jnp.exp2(before - top)
    highs, lows, total = [], [], None
    for s in parts:
        p = jnp.exp2(s - top)
        total = p if total is None else total + p
        high, rest = halves(p)
        highs.append(high)
        lows.append(rest)
    mixed = jnp.dot(jnp.concatenate(highs + lows, axis=1), v_buf[...], preferred_element_type=F32)
    mixed = mixed[:, 0:128] + mixed[:, 128:256]
    if first:
        l_ref[rows, :] = total
        acc_ref[rows, :] = mixed
    else:
        l_ref[rows, :] = l_ref[rows, :] * shrink + total
        acc_ref[rows, :] = acc_ref[rows, :] * shrink + mixed
    m_ref[rows, :] = top


def own_kernel(heads, info, lens_ref, q_ref, mine_ref, other_ref, acc_ref, m_ref, l_ref, q_buf, qs_ref, low_ref, k_buf, v_buf):
    index = info[0]
    rows = q_ref.shape[0]
    tokens = rows // heads
    core = index % 2
    base = (index - core) * tokens
    place(mine_ref, core * tokens, k_buf, v_buf)
    place(other_ref, (1 - core) * tokens, k_buf, v_buf)
    high, low = halves(q_ref[...] * (math.log2(math.e) / math.sqrt(q_ref.shape[1])))
    q_buf[:, 0:128] = high
    q_buf[:, 128:256] = low
    docs = lens_ref.shape[0]
    lens = lens_ref[...]
    ahead = lax.broadcasted_iota(jnp.int32, (docs, docs), 0) < lax.broadcasted_iota(jnp.int32, (docs, docs), 1)
    starts = jnp.sum(jnp.where(ahead, jnp.broadcast_to(lens, (docs, docs)), 0), axis=0, keepdims=True)

    def find(i, carry):
        at = pl.ds(pl.multiple_of(i * 256, 256), 256)
        row = lax.broadcasted_iota(jnp.int32, (256, docs), 0) + i * 256
        pos = index * tokens + row // heads
        begun = jnp.where(starts <= pos, jnp.broadcast_to(starts, pos.shape), 0)
        start = jnp.max(begun.astype(F32), axis=1, keepdims=True).astype(jnp.int32)
        qs_ref[at, :] = jnp.broadcast_to(start, (256, 128))
        return carry

    lax.fori_loop(0, rows // 256, find, 0)
    for tile in range(rows // (TILE * heads)):
        low_ref[tile] = jnp.max(qs_ref[tile * TILE * heads : tile * TILE * heads + 8, :])

    def tile_body(tile, carry):
        for part in range(TILE * heads // CHUNK):
            begin = tile * (TILE * heads) + part * CHUNK
            at = pl.ds(pl.multiple_of(begin, CHUNK), CHUNK)
            row = lax.broadcasted_iota(jnp.int32, (CHUNK, 128), 0) + begin
            row_pos = index * tokens + row // heads
            step(at, True, True, base, q_buf, k_buf, v_buf, qs_ref, acc_ref, m_ref, l_ref, row_pos)
        return carry

    lax.fori_loop(0, rows // (TILE * heads), tile_body, 0)


def back_kernel(heads, distance, last, info, low_ref, mine_ref, other_ref, q_buf, qs_ref, acc_in, m_in, l_in, *rest):
    if last:
        out_ref, k_buf, v_buf = rest
        acc_ref, m_ref, l_ref = acc_in, m_in, l_in
    else:
        acc_ref, m_ref, l_ref, k_buf, v_buf = rest
    index = info[0]
    rows = q_buf.shape[0]
    tokens = rows // heads
    core = index % 2
    base = (index - core - 2 * distance) * tokens
    end = base + 2 * tokens

    @pl.when(low_ref[0] < end)
    def _():
        place(mine_ref, core * tokens, k_buf, v_buf)
        place(other_ref, (1 - core) * tokens, k_buf, v_buf)

    def tile_body(tile, carry):
        @pl.when(low_ref[tile] < end)
        def _():
            for part in range(TILE * heads // CHUNK):
                at = pl.ds(pl.multiple_of(tile * (TILE * heads) + part * CHUNK, CHUNK), CHUNK)
                step(at, False, False, base, q_buf, k_buf, v_buf, qs_ref, acc_ref, m_ref, l_ref, None)

        return carry

    lax.fori_loop(0, rows // (TILE * heads), tile_body, 0)
    if last:
        out_ref[...] = acc_ref[...] / jnp.sum(l_ref[...], axis=1, keepdims=True)


VMEM = pl.BlockSpec(memory_space=pltpu.VMEM)
SMEM = pl.BlockSpec(memory_space=pltpu.SMEM)
LIMIT = 24 << 20


def buffers(tokens):
    return [pltpu.VMEM((2 * tokens, 384), BF16), pltpu.VMEM((4 * tokens, 256), BF16)]


def attend_own(heads, info, lens, q, mine, other):
    rows = q.shape[0]
    tokens = rows // heads
    full = jax.ShapeDtypeStruct((rows, 128), F32)
    return pl.pallas_call(
        functools.partial(own_kernel, heads),
        name="own_pair",
        out_shape=(
            full,
            full,
            full,
            jax.ShapeDtypeStruct((rows, 256), BF16),
            jax.ShapeDtypeStruct((rows, 128), jnp.int32),
            jax.ShapeDtypeStruct((rows // (TILE * heads),), jnp.int32),
        ),
        in_specs=[SMEM, VMEM, VMEM, VMEM, VMEM],
        out_specs=(VMEM, VMEM, VMEM, VMEM, VMEM, SMEM),
        scratch_shapes=buffers(tokens),
        compiler_params=pltpu.CompilerParams(vmem_limit_bytes=LIMIT),
    )(info, lens, q, mine, other)


def attend_back(heads, distance, last, info, low, mine, other, q_buf, qs, state):
    rows = q_buf.shape[0]
    tokens = rows // heads
    full = jax.ShapeDtypeStruct((rows, 128), F32)
    return pl.pallas_call(
        functools.partial(back_kernel, heads, distance, last),
        name=f"back_{distance}",
        out_shape=full if last else (full, full, full),
        in_specs=[SMEM, SMEM] + [VMEM] * 7,
        out_specs=VMEM if last else (VMEM, VMEM, VMEM),
        input_output_aliases={} if last else {6: 0, 7: 1, 8: 2},
        scratch_shapes=buffers(tokens),
        compiler_params=pltpu.CompilerParams(vmem_limit_bytes=LIMIT),
    )(info, low, mine, other, q_buf, qs, *state)


def on_device(queries, key_rows, value_rows, doc_lengths):
    tokens, heads, width = queries.shape
    count = lax.axis_size(AXES)
    index = lax.axis_index(AXES).astype(jnp.int32)
    info = jnp.reshape(index, (1,))
    q = queries.reshape(tokens * heads, width)
    lens = doc_lengths.reshape(-1, 1)
    ahead = [(i, i + 2) for i in range(count - 2)]
    swap = [(i, i ^ 1) for i in range(count)]
    held = jnp.concatenate([key_rows, value_rows], axis=0)
    partner = lax.ppermute(held, AXES, swap)
    *state, q_buf, qs, low = attend_own(heads, info, lens, q, held, partner)
    pairs = REACH // 2
    held = lax.ppermute(held, AXES, ahead)
    for distance in range(1, pairs + 1):
        held, *state = lax.optimization_barrier((held, *state))
        following = lax.ppermute(held, AXES, ahead) if distance < pairs else None
        partner = lax.ppermute(held, AXES, swap)
        state = attend_back(heads, distance, distance == pairs, info, low, held, partner, q_buf, qs, state)
        held = following
    return state.reshape(tokens, heads, width)


def solution(mesh):
    in_specs = (P(AXES, None, None), P(AXES, None), P(AXES, None), P())
    return jax.shard_map(
        on_device, mesh=mesh, in_specs=in_specs, out_specs=P(AXES, None, None), check_vma=False
    )
```

```python
import functools
import math

import jax
import jax.numpy as jnp
from jax import lax
from jax.experimental import pallas as pl
from jax.experimental.pallas import tpu as pltpu
from jax.sharding import PartitionSpec as P

AXES = ("inner", "outer")
REACH = 8
NEGATIVE = -1e30
TILE = 128
CHUNK = 256
BF16 = jnp.bfloat16
F32 = jnp.float32


def halves(x):
    high = x.astype(BF16)
    return high, (x - high.astype(F32)).astype(BF16)


def place(kv_ref, start, k_buf, v_buf):
    rows = kv_ref.shape[0] // 2
    at = pl.ds(pl.multiple_of(start, 128), rows)
    high, low = halves(kv_ref[0:rows, :])
    k_buf[at, 0:128] = high
    k_buf[at, 128:256] = high
    k_buf[at, 256:384] = low
    high, low = halves(kv_ref[rows : 2 * rows, :])
    for turn in range(2):
        at = pl.ds(pl.multiple_of(start + turn * 2 * rows, 128), rows)
        v_buf[at, 0:128] = high
        v_buf[at, 128:256] = low


def step(rows, first, own, base, q_buf, k_buf, v_buf, qs_ref, acc_ref, m_ref, l_ref, row_pos):
    keys = k_buf.shape[0]
    nt = (((1,), (1,)), ((), ()))
    q_all = q_buf[rows, :]
    scores = lax.dot_general(q_all, k_buf[:, 0:256], nt, preferred_element_type=F32)
    scores += lax.dot_general(q_all[:, 0:128], k_buf[:, 256:384], nt, preferred_element_type=F32)
    low = qs_ref[rows, :] - base
    lane = lax.broadcasted_iota(jnp.int32, low.shape, 1)
    parts = []
    for c in range(keys // 128):
        s = scores[:, c * 128 : (c + 1) * 128]
        allowed = lane + c * 128 >= low
        if own:
            allowed &= lane + c * 128 <= row_pos - base
        parts.append(jnp.where(allowed, s, NEGATIVE))
    top = functools.reduce(jnp.maximum, parts)
    top = jnp.broadcast_to(jnp.max(top, axis=1, keepdims=True), top.shape)
    if not first:
        before = m_ref[rows, :]
        top = jnp.maximum(before, top)
        shrink = jnp.exp2(before - top)
    highs, lows, total = [], [], None
    for s in parts:
        p = jnp.exp2(s - top)
        total = p if total is None else total + p
        high, rest = halves(p)
        highs.append(high)
        lows.append(rest)
    mixed = jnp.dot(jnp.concatenate(highs + lows, axis=1), v_buf[...], preferred_element_type=F32)
    mixed = mixed[:, 0:128] + mixed[:, 128:256]
    if first:
        l_ref[rows, :] = total
        acc_ref[rows, :] = mixed
    else:
        l_ref[rows, :] = l_ref[rows, :] * shrink + total
        acc_ref[rows, :] = acc_ref[rows, :] * shrink + mixed
    m_ref[rows, :] = top


def own_kernel(heads, info, lens_ref, q_hbm, mine_ref, other_ref, acc_ref, m_ref, l_ref, q_buf, qs_ref, low_ref, k_buf, v_buf, q_ref, sem):
    fetch = pltpu.make_async_copy(q_hbm, q_ref, sem)
    fetch.start()
    index = info[0]
    rows = q_ref.shape[0]
    tokens = rows // heads
    core = index % 2
    base = (index - core) * tokens
    place(mine_ref, core * tokens, k_buf, v_buf)
    place(other_ref, (1 - core) * tokens, k_buf, v_buf)
    docs = lens_ref.shape[1]
    lens = jnp.broadcast_to(lens_ref[...], (8, docs))
    ahead = lax.broadcasted_iota(jnp.int32, (docs, docs), 0) < lax.broadcasted_iota(jnp.int32, (docs, docs), 1)
    ahead = ahead.astype(F32).astype(BF16)
    coarse = jnp.dot((lens // 64).astype(F32).astype(BF16), ahead, preferred_element_type=F32)
    fine = jnp.dot((lens % 64).astype(F32).astype(BF16), ahead, preferred_element_type=F32)
    starts = (coarse * 64.0 + fine)[0:1, :]

    def find(i, carry):
        at = pl.ds(pl.multiple_of(i * 256, 256), 256)
        row = lax.broadcasted_iota(jnp.int32, (256, docs), 0) + i * 256
        pos = index * tokens + row // heads
        begun = jnp.where(starts <= pos.astype(F32), jnp.broadcast_to(starts, pos.shape), 0.0)
        start = jnp.max(begun, axis=1, keepdims=True).astype(jnp.int32)
        qs_ref[at, :] = jnp.broadcast_to(start, (256, 128))
        return carry

    lax.fori_loop(0, rows // 256, find, 0)
    for tile in range(rows // (TILE * heads)):
        low_ref[tile] = jnp.max(qs_ref[tile * TILE * heads : tile * TILE * heads + 8, :])

    fetch.wait()
    high, low = halves(q_ref[...] * (math.log2(math.e) / math.sqrt(q_ref.shape[1])))
    q_buf[:, 0:128] = high
    q_buf[:, 128:256] = low

    def tile_body(tile, carry):
        for part in range(TILE * heads // CHUNK):
            begin = tile * (TILE * heads) + part * CHUNK
            at = pl.ds(pl.multiple_of(begin, CHUNK), CHUNK)
            row = lax.broadcasted_iota(jnp.int32, (CHUNK, 128), 0) + begin
            row_pos = index * tokens + row // heads
            step(at, True, True, base, q_buf, k_buf, v_buf, qs_ref, acc_ref, m_ref, l_ref, row_pos)
        return carry

    lax.fori_loop(0, rows // (TILE * heads), tile_body, 0)


def back_kernel(heads, units, last, info, low_ref, q_buf, qs_ref, acc_in, m_in, l_in, *rest):
    pieces, rest = rest[: 2 * len(units)], rest[2 * len(units) :]
    if last:
        out_ref, k_buf, v_buf = rest
        acc_ref, m_ref, l_ref = acc_in, m_in, l_in
    else:
        acc_ref, m_ref, l_ref, k_buf, v_buf = rest
    index = info[0]
    rows = q_buf.shape[0]
    tokens = rows // heads
    core = index % 2
    odd = index // 2 % 2
    for n, (even_distance, odd_distance) in enumerate(units):
        mine_ref, other_ref = pieces[2 * n : 2 * n + 2]
        base = (index - core - 2 * jnp.where(odd == 0, even_distance, odd_distance)) * tokens
        end = base + 2 * tokens
        if even_distance == 0 or odd_distance == 0:
            end = jnp.where(odd == (1 if even_distance == 0 else 0), end, -1)

        @pl.when(low_ref[0] < end)
        def _():
            place(mine_ref, core * tokens, k_buf, v_buf)
            place(other_ref, (1 - core) * tokens, k_buf, v_buf)

        def tile_body(tile, carry):
            @pl.when(low_ref[tile] < end)
            def _():
                for part in range(TILE * heads // CHUNK):
                    at = pl.ds(pl.multiple_of(tile * (TILE * heads) + part * CHUNK, CHUNK), CHUNK)
                    step(at, False, False, base, q_buf, k_buf, v_buf, qs_ref, acc_ref, m_ref, l_ref, None)

            return carry

        lax.fori_loop(0, rows // (TILE * heads), tile_body, 0)
    if last:
        out_ref[...] = acc_ref[...] / jnp.sum(l_ref[...], axis=1, keepdims=True)


VMEM = pl.BlockSpec(memory_space=pltpu.VMEM)
SMEM = pl.BlockSpec(memory_space=pltpu.SMEM)
LIMIT = 24 << 20


def buffers(tokens):
    return [pltpu.VMEM((2 * tokens, 384), BF16), pltpu.VMEM((4 * tokens, 256), BF16)]


def attend_own(heads, info, lens, q, mine, other):
    rows = q.shape[0]
    tokens = rows // heads
    full = jax.ShapeDtypeStruct((rows, 128), F32)
    return pl.pallas_call(
        functools.partial(own_kernel, heads),
        name="own_pair",
        out_shape=(
            full,
            full,
            full,
            jax.ShapeDtypeStruct((rows, 256), BF16),
            jax.ShapeDtypeStruct((rows, 128), jnp.int32),
            jax.ShapeDtypeStruct((rows // (TILE * heads),), jnp.int32),
        ),
        in_specs=[SMEM, VMEM, pl.BlockSpec(memory_space=pltpu.HBM), VMEM, VMEM],
        out_specs=(VMEM, VMEM, VMEM, VMEM, VMEM, SMEM),
        scratch_shapes=buffers(tokens) + [pltpu.VMEM((rows, 128), F32), pltpu.SemaphoreType.DMA],
        compiler_params=pltpu.CompilerParams(vmem_limit_bytes=LIMIT),
    )(info, lens, q, mine, other)


def attend_back(name, heads, units, last, info, low, q_buf, qs, state, pieces):
    rows = q_buf.shape[0]
    tokens = rows // heads
    full = jax.ShapeDtypeStruct((rows, 128), F32)
    return pl.pallas_call(
        functools.partial(back_kernel, heads, units, last),
        name=name,
        out_shape=full if last else (full, full, full),
        in_specs=[SMEM, SMEM] + [VMEM] * (5 + len(pieces)),
        out_specs=VMEM if last else (VMEM, VMEM, VMEM),
        input_output_aliases={} if last else {4: 0, 5: 1, 6: 2},
        scratch_shapes=buffers(tokens),
        compiler_params=pltpu.CompilerParams(vmem_limit_bytes=LIMIT),
    )(info, low, q_buf, qs, *state, *pieces)


def on_device(queries, key_rows, value_rows, doc_lengths):
    tokens, heads, width = queries.shape
    count = lax.axis_size(AXES)
    index = lax.axis_index(AXES).astype(jnp.int32)
    info = jnp.reshape(index, (1,))
    q = pltpu.with_memory_space_constraint(queries.reshape(tokens * heads, width), pltpu.HBM)
    lens = doc_lengths.reshape(1, -1)
    devices = range(count)
    even = [i for i in devices if i // 2 % 2 == 0]
    odd = [i for i in devices if i // 2 % 2 == 1]

    def send(x, pairs):
        return lax.ppermute(x, AXES, pairs)

    def partner(x, among=devices):
        return send(x, [(i, i ^ 1) for i in among])

    up = [(i, i + 4) for i in devices if i + 4 < count]
    held = jnp.stack([key_rows, value_rows]).reshape(2 * tokens, width)
    held_other = partner(held)
    up_1 = send(held, up)
    across_1 = send(held, [(i, i + 2) for i in even])
    *state, q_buf, qs, low = attend_own(heads, info, lens, q, held, held_other)
    up_1, across_1, *state = lax.optimization_barrier((up_1, across_1, *state))
    up_2 = send(up_1, up)
    across_2 = send(up_1, [(i, i ^ 2) for i in devices])
    pieces = (up_1, partner(up_1), across_1, partner(across_1, odd))
    state = attend_back("phase_1", heads, ((2, 2), (0, 1)), False, info, low, q_buf, qs, state, pieces)
    up_2, across_2, *state = lax.optimization_barrier((up_2, across_2, *state))
    across_3 = send(up_2, [(i, i - 2) for i in odd])
    pieces = (across_2, partner(across_2), up_2, partner(up_2))
    state = attend_back("phase_2", heads, ((1, 3), (4, 4)), False, info, low, q_buf, qs, state, pieces)
    across_3, *state = lax.optimization_barrier((across_3, *state))
    pieces = (across_3, partner(across_3, even))
    out = attend_back("phase_3", heads, ((3, 0),), True, info, low, q_buf, qs, state, pieces)
    return out.reshape(tokens, heads, width)


def solution(mesh):
    in_specs = (P(AXES, None, None), P(AXES, None), P(AXES, None), P())
    return jax.shard_map(
        on_device, mesh=mesh, in_specs=in_specs, out_specs=P(AXES, None, None), check_vma=False
    )
```

```python
import functools
import math

import jax
import jax.numpy as jnp
from jax import lax
from jax.experimental import pallas as pl
from jax.experimental.pallas import tpu as pltpu
from jax.sharding import PartitionSpec as P

AXES = ("inner", "outer")
REACH = 8
NEGATIVE = -1e30
TILE = 128
WINDOW = 256
CHUNK = 256
BF16 = jnp.bfloat16
F32 = jnp.float32


def halves(x):
    high = x.astype(BF16)
    return high, (x - high.astype(F32)).astype(BF16)


def place(kv_ref, start, k_buf, v_buf):
    rows = kv_ref.shape[0] // 2
    at = pl.ds(pl.multiple_of(start, 128), rows)
    for source, target in ((kv_ref[0:rows, :], k_buf), (kv_ref[rows : 2 * rows, :], v_buf)):
        high, low = halves(source)
        target[at, 0:128] = high
        target[at, 128:256] = low


def fill_lanes(lane_ref):
    lane_ref[...] = lax.broadcasted_iota(jnp.int32, lane_ref.shape, 1)


def spread(ref, lanes, rows):
    x = ref[0:8, lanes]
    return jnp.broadcast_to(x[None], (rows // 8,) + x.shape).reshape(rows, x.shape[1])


def step(rows, q_all, window, row_pos, base, k_buf, v_buf, lane_ref, qs_ref, acc_ref, m_ref, l_ref):
    first = row_pos is not None
    keys = slice(*window)
    nt = (((1,), (1,)), ((), ()))
    k_high = k_buf[keys, 0:128]
    scores = lax.dot_general(q_all, jnp.concatenate([k_high, k_high], axis=1), nt, preferred_element_type=F32)
    scores += lax.dot_general(q_all[:, 0:128], k_buf[keys, 128:256], nt, preferred_element_type=F32)
    low = qs_ref[rows, :] - base
    if first:
        low = low - jnp.int32(-(2**31))
        bound = row_pos - base - low
    parts = []
    for c in range((window[1] - window[0]) // 128):
        s = scores[:, c * 128 : (c + 1) * 128]
        lane = spread(lane_ref, slice(window[0] + c * 128, window[0] + (c + 1) * 128), s.shape[0])
        allowed = lane - low <= bound if first else lane >= low
        parts.append(jnp.where(allowed, s, NEGATIVE))
    top = functools.reduce(jnp.maximum, parts)
    top = jnp.broadcast_to(jnp.max(top, axis=1, keepdims=True), top.shape)
    if not first:
        before = m_ref[rows, :]
        top = jnp.maximum(before, top)
        shrink = jnp.exp2(before - top)
    highs, lows, total = [], [], None
    for s in parts:
        p = jnp.exp2(s - top)
        total = p if total is None else total + p
        high, rest = halves(p)
        highs.append(high)
        lows.append(rest)
    values = v_buf[keys, :]
    values = jnp.concatenate([values, values], axis=0)
    mixed = jnp.dot(jnp.concatenate(highs + lows, axis=1), values, preferred_element_type=F32)
    mixed = mixed[:, 0:128] + mixed[:, 128:256]
    if first:
        l_ref[rows, :] = total
        acc_ref[rows, :] = mixed
    else:
        l_ref[rows, :] = l_ref[rows, :] * shrink + total
        acc_ref[rows, :] = acc_ref[rows, :] * shrink + mixed
    m_ref[rows, :] = top


def chunks(tile, size):
    for part in range(size // CHUNK):
        begin = tile * size + part * CHUNK
        yield begin, pl.ds(pl.multiple_of(begin, CHUNK), CHUNK)


def own_kernel(heads, info, lens_ref, q_hbm, mine_ref, other_ref, acc_ref, m_ref, l_ref, q_buf, qs_ref, low_ref, *scratch):
    k_buf, v_buf, lane_ref, q_ref, sem = scratch
    fetch = pltpu.make_async_copy(q_hbm, q_ref, sem)
    fetch.start()
    index = info[0]
    rows = q_ref.shape[0]
    tokens = rows // heads
    core = index % 2
    base = (index - core) * tokens
    place(mine_ref, core * tokens, k_buf, v_buf)
    place(other_ref, (1 - core) * tokens, k_buf, v_buf)
    docs = lens_ref.shape[1]
    lens = jnp.broadcast_to(lens_ref[...], (8, docs))
    ahead = lax.broadcasted_iota(jnp.int32, (docs, docs), 0) < lax.broadcasted_iota(jnp.int32, (docs, docs), 1)
    ahead = ahead.astype(F32).astype(BF16)
    coarse = jnp.dot((lens // 64).astype(F32).astype(BF16), ahead, preferred_element_type=F32)
    fine = jnp.dot((lens % 64).astype(F32).astype(BF16), ahead, preferred_element_type=F32)
    starts = (coarse * 64.0 + fine)[0:1, :]
    pos = lax.broadcasted_iota(jnp.int32, (tokens, docs), 0) + index * tokens
    begun = jnp.where(starts <= pos.astype(F32), jnp.broadcast_to(starts, pos.shape), 0.0)
    start = jnp.max(begun, axis=1, keepdims=True).astype(jnp.int32)
    start = jnp.broadcast_to(jnp.broadcast_to(start, (tokens, 128))[:, None, :], (tokens, heads, 128))
    qs_ref[...] = start.reshape(rows, 128)
    fill_lanes(lane_ref)
    size = TILE * heads
    for tile in range(rows // size):
        low_ref[tile] = jnp.max(qs_ref[tile * size : tile * size + 8, :])
    fetch.wait()
    short = 512

    def tile_body(tile, carry):
        def attend(window):
            for begin, at in chunks(tile, size):
                high, low = halves(q_ref[at, :] * (math.log2(math.e) / math.sqrt(q_ref.shape[1])))
                q_all = jnp.concatenate([high, low], axis=1)
                q_buf[at, :] = q_all
                row = lax.broadcasted_iota(jnp.int32, (CHUNK, 128), 0) + begin
                step(at, q_all, window, index * tokens + row // heads, base, k_buf, v_buf, lane_ref, qs_ref, acc_ref, m_ref, l_ref)

        fits = core * tokens + (tile + 1) * TILE <= short
        pl.when(fits)(lambda: attend((0, short)))
        pl.when(jnp.logical_not(fits))(lambda: attend((0, 2 * tokens)))
        return carry

    lax.fori_loop(0, rows // size, tile_body, 0)


def back_kernel(heads, units, last, info, low_ref, q_buf, qs_ref, acc_in, m_in, l_in, *rest):
    pieces, rest = rest[: 2 * len(units)], rest[2 * len(units) :]
    if last:
        out_hbm, k_buf, v_buf, lane_ref, out_ref, sems = rest
        acc_ref, m_ref, l_ref = acc_in, m_in, l_in
    else:
        acc_ref, m_ref, l_ref, k_buf, v_buf, lane_ref = rest
    index = info[0]
    rows = q_buf.shape[0]
    tokens = rows // heads
    size = TILE * heads
    core = index % 2
    odd = index // 2 % 2
    fill_lanes(lane_ref)

    def unit_body(n, carry):
        distance = jnp.int32(0)
        for m, (even_distance, odd_distance) in enumerate(units):
            chosen = jnp.where(odd == 0, even_distance, odd_distance)
            distance = jnp.where(n == m, chosen, distance)
        base = (index - core - 2 * distance) * tokens
        end = jnp.where(distance > 0, base + 2 * tokens, -1)
        for m in range(len(units)):

            @pl.when((n == m) & (low_ref[0] < end))
            def _():
                place(pieces[2 * m], core * tokens, k_buf, v_buf)
                place(pieces[2 * m + 1], (1 - core) * tokens, k_buf, v_buf)

        def tile_body(tile, carry):
            skip = low_ref[tile] - base
            for begin in range(0, 2 * tokens, WINDOW):
                reached = skip < begin + WINDOW
                if begin:
                    reached &= skip >= begin

                @pl.when((low_ref[tile] < end) & reached)
                def _():
                    for _, at in chunks(tile, size):
                        step(at, q_buf[at, :], (begin, 2 * tokens), None, base, k_buf, v_buf, lane_ref, qs_ref, acc_ref, m_ref, l_ref)

            return carry

        lax.fori_loop(0, rows // size, tile_body, 0)
        return carry

    lax.fori_loop(0, len(units), unit_body, 0)
    if last:
        copies = []
        for part in range(rows // CHUNK):
            at = slice(part * CHUNK, (part + 1) * CHUNK)
            out_ref[at, :] = acc_ref[at, :] / jnp.sum(l_ref[at, :], axis=1, keepdims=True)
            copies.append(pltpu.make_async_copy(out_ref.at[at], out_hbm.at[at], sems.at[part]))
            copies[-1].start()
        for copy in copies:
            copy.wait()


VMEM = pl.BlockSpec(memory_space=pltpu.VMEM)
SMEM = pl.BlockSpec(memory_space=pltpu.SMEM)
HBM = pl.BlockSpec(memory_space=pltpu.HBM)
LIMIT = 24 << 20


def buffers(tokens):
    split = pltpu.VMEM((2 * tokens, 256), BF16)
    return [split, split, pltpu.VMEM((8, 2 * tokens), jnp.int32)]


def attend_own(heads, info, lens, q, mine, other):
    rows = q.shape[0]
    tokens = rows // heads
    full = jax.ShapeDtypeStruct((rows, 128), F32)
    return pl.pallas_call(
        functools.partial(own_kernel, heads),
        name="own_pair",
        out_shape=(
            full,
            full,
            full,
            jax.ShapeDtypeStruct((rows, 256), BF16),
            jax.ShapeDtypeStruct((rows, 128), jnp.int32),
            jax.ShapeDtypeStruct((rows // (TILE * heads),), jnp.int32),
        ),
        in_specs=[SMEM, VMEM, HBM, VMEM, VMEM],
        out_specs=(VMEM, VMEM, VMEM, VMEM, VMEM, SMEM),
        scratch_shapes=buffers(tokens) + [pltpu.VMEM((rows, 128), F32), pltpu.SemaphoreType.DMA],
        compiler_params=pltpu.CompilerParams(vmem_limit_bytes=LIMIT),
    )(info, lens, q, mine, other)


def attend_back(name, heads, units, last, info, low, q_buf, qs, state, pieces):
    rows = q_buf.shape[0]
    tokens = rows // heads
    full = jax.ShapeDtypeStruct((rows, 128), F32)
    tail = [pltpu.VMEM((rows, 128), F32), pltpu.SemaphoreType.DMA((rows // CHUNK,))]
    return pl.pallas_call(
        functools.partial(back_kernel, heads, units, last),
        name=name,
        out_shape=full if last else (full, full, full),
        in_specs=[SMEM, SMEM] + [VMEM] * (5 + len(pieces)),
        out_specs=HBM if last else (VMEM, VMEM, VMEM),
        input_output_aliases={} if last else {4: 0, 5: 1, 6: 2},
        scratch_shapes=buffers(tokens) + (tail if last else []),
        compiler_params=pltpu.CompilerParams(vmem_limit_bytes=LIMIT),
    )(info, low, q_buf, qs, *state, *pieces)


def on_device(queries, key_rows, value_rows, doc_lengths):
    tokens, heads, width = queries.shape
    count = lax.axis_size(AXES)
    index = lax.axis_index(AXES).astype(jnp.int32)
    info = jnp.reshape(index, (1,))
    q = pltpu.with_memory_space_constraint(queries.reshape(tokens * heads, width), pltpu.HBM)
    lens = doc_lengths.reshape(1, -1)
    devices = range(count)
    even = [i for i in devices if i // 2 % 2 == 0]
    odd = [i for i in devices if i // 2 % 2 == 1]

    def send(x, pairs):
        return lax.ppermute(x, AXES, pairs)

    def partner(x, among=devices):
        return send(x, [(i, i ^ 1) for i in among])

    up = [(i, i + 4) for i in devices if i + 4 < count]
    held = jnp.stack([key_rows, value_rows]).reshape(2 * tokens, width)
    held_other = partner(held)
    up_1 = send(held, up)
    across_1 = send(held, [(i, i + 2) for i in even])
    *state, q_buf, qs, low = attend_own(heads, info, lens, q, held, held_other)
    up_1, across_1, *state = lax.optimization_barrier((up_1, across_1, *state))
    up_2 = send(up_1, up)
    across_2 = send(up_1, [(i, i ^ 2) for i in devices])
    pieces = (up_1, partner(up_1), across_1, partner(across_1, odd))
    state = attend_back("phase_1", heads, ((2, 2), (0, 1)), False, info, low, q_buf, qs, state, pieces)
    up_2, across_2, *state = lax.optimization_barrier((up_2, across_2, *state))
    across_3 = send(up_2, [(i, i - 2) for i in odd])
    pieces = (across_2, partner(across_2), up_2, partner(up_2))
    state = attend_back("phase_2", heads, ((1, 3), (4, 4)), False, info, low, q_buf, qs, state, pieces)
    across_3, *state = lax.optimization_barrier((across_3, *state))
    pieces = (across_3, partner(across_3, even))
    out = attend_back("phase_3", heads, ((3, 0),), True, info, low, q_buf, qs, state, pieces)
    return out.reshape(tokens, heads, width)


def solution(mesh):
    in_specs = (P(AXES, None, None), P(AXES, None), P(AXES, None), P())
    return jax.shard_map(
        on_device, mesh=mesh, in_specs=in_specs, out_specs=P(AXES, None, None), check_vma=False
    )
```

```python
import functools
import math

import jax
import jax.numpy as jnp
from jax import lax
from jax.experimental import pallas as pl
from jax.experimental.pallas import tpu as pltpu
from jax.sharding import PartitionSpec as P

AXES = ("inner", "outer")
NEGATIVE = -1e30
TILE = 128
WINDOW = 256
CHUNK = 256
BF16 = jnp.bfloat16
F32 = jnp.float32


def halves(x):
    high = x.astype(BF16)
    return high, (x - high.astype(F32)).astype(BF16)


def place(kv_ref, start, k_buf, v_buf):
    rows = kv_ref.shape[0] // 2
    at = pl.ds(pl.multiple_of(start, 128), rows)
    for source, target in ((kv_ref[0:rows, :], k_buf), (kv_ref[rows : 2 * rows, :], v_buf)):
        high, low = halves(source)
        target[at, 0:128] = high
        target[at, 128:256] = low


def fill_lanes(lane_ref):
    lane_ref[...] = lax.broadcasted_iota(jnp.int32, lane_ref.shape, 1)


def spread(ref, lanes, rows):
    x = ref[0:8, lanes]
    return jnp.broadcast_to(x[None], (rows // 8,) + x.shape).reshape(rows, x.shape[1])


def step(rows, q_all, window, row_pos, base, k_buf, v_buf, lane_ref, qs_ref, acc_ref, m_ref, l_ref):
    first = row_pos is not None
    keys = slice(*window)
    nt = (((1,), (1,)), ((), ()))
    k_high = k_buf[keys, 0:128]
    scores = lax.dot_general(q_all, jnp.concatenate([k_high, k_high], axis=1), nt, preferred_element_type=F32)
    scores += lax.dot_general(q_all[:, 0:128], k_buf[keys, 128:256], nt, preferred_element_type=F32)
    low = qs_ref[rows, :] - base
    if first:
        low = low - jnp.int32(-(2**31))
        bound = row_pos - base - low
    parts = []
    for c in range((window[1] - window[0]) // 128):
        s = scores[:, c * 128 : (c + 1) * 128]
        lane = spread(lane_ref, slice(window[0] + c * 128, window[0] + (c + 1) * 128), s.shape[0])
        allowed = lane - low <= bound if first else lane >= low
        parts.append(jnp.where(allowed, s, NEGATIVE))
    top = functools.reduce(jnp.maximum, parts)
    top = jnp.broadcast_to(jnp.max(top, axis=1, keepdims=True), top.shape)
    if not first:
        before = m_ref[rows, :]
        top = jnp.maximum(before, top)
        shrink = jnp.exp2(before - top)
    highs, lows, total = [], [], None
    for s in parts:
        p = jnp.exp2(s - top)
        total = p if total is None else total + p
        high, rest = halves(p)
        highs.append(high)
        lows.append(rest)
    values = v_buf[keys, :]
    values = jnp.concatenate([values, values], axis=0)
    mixed = jnp.dot(jnp.concatenate(highs + lows, axis=1), values, preferred_element_type=F32)
    mixed = mixed[:, 0:128] + mixed[:, 128:256]
    if first:
        l_ref[rows, :] = total
        acc_ref[rows, :] = mixed
    else:
        l_ref[rows, :] = l_ref[rows, :] * shrink + total
        acc_ref[rows, :] = acc_ref[rows, :] * shrink + mixed
    m_ref[rows, :] = top


def chunks(tile, size):
    for part in range(size // CHUNK):
        begin = tile * size + part * CHUNK
        yield begin, pl.ds(pl.multiple_of(begin, CHUNK), CHUNK)


def own_kernel(heads, info, lens_hbm, q_hbm, mine_ref, other_ref, acc_ref, m_ref, l_ref, q_buf, qs_ref, low_ref, *scratch):
    k_buf, v_buf, lane_ref, q_ref, lens_ref, sems = scratch
    fetch_lens = pltpu.make_async_copy(lens_hbm, lens_ref, sems.at[0])
    fetch_lens.start()
    fetch = pltpu.make_async_copy(q_hbm, q_ref, sems.at[1])
    fetch.start()
    index = info[0]
    rows = q_ref.shape[0]
    tokens = rows // heads
    core = index % 2
    base = (index - core) * tokens
    place(mine_ref, core * tokens, k_buf, v_buf)
    place(other_ref, (1 - core) * tokens, k_buf, v_buf)
    fetch_lens.wait()
    docs = lens_ref.shape[1]
    lens = jnp.broadcast_to(lens_ref[...], (8, docs))
    ahead = lax.broadcasted_iota(jnp.int32, (docs, docs), 0) < lax.broadcasted_iota(jnp.int32, (docs, docs), 1)
    ahead = ahead.astype(F32).astype(BF16)
    coarse = jnp.dot((lens // 64).astype(F32).astype(BF16), ahead, preferred_element_type=F32)
    fine = jnp.dot((lens % 64).astype(F32).astype(BF16), ahead, preferred_element_type=F32)
    starts = (coarse * 64.0 + fine)[0:1, :]
    pos = lax.broadcasted_iota(jnp.int32, (tokens, docs), 0) + index * tokens
    begun = jnp.where(starts <= pos.astype(F32), jnp.broadcast_to(starts, pos.shape), 0.0)
    start = jnp.max(begun, axis=1, keepdims=True).astype(jnp.int32)
    start = jnp.broadcast_to(jnp.broadcast_to(start, (tokens, 128))[:, None, :], (tokens, heads, 128))
    qs_ref[...] = start.reshape(rows, 128)
    fill_lanes(lane_ref)
    size = TILE * heads
    for tile in range(rows // size):
        low_ref[tile] = jnp.max(qs_ref[tile * size : tile * size + 8, :])
    fetch.wait()
    short = 512

    def tile_body(tile, carry):
        def attend(window):
            for begin, at in chunks(tile, size):
                high, low = halves(q_ref[at, :] * (math.log2(math.e) / math.sqrt(q_ref.shape[1])))
                q_all = jnp.concatenate([high, low], axis=1)
                q_buf[at, :] = q_all
                row = lax.broadcasted_iota(jnp.int32, (CHUNK, 128), 0) + begin
                step(at, q_all, window, index * tokens + row // heads, base, k_buf, v_buf, lane_ref, qs_ref, acc_ref, m_ref, l_ref)

        fits = core * tokens + (tile + 1) * TILE <= short
        pl.when(fits)(lambda: attend((0, short)))
        pl.when(jnp.logical_not(fits))(lambda: attend((0, 2 * tokens)))
        return carry

    lax.fori_loop(0, rows // size, tile_body, 0)


def back_kernel(heads, distances, last, info, low_ref, q_buf, qs_ref, acc_in, m_in, l_in, mine_ref, other_ref, *rest):
    if last:
        out_hbm, k_buf, v_buf, lane_ref, out_ref, sems = rest
        acc_ref, m_ref, l_ref = acc_in, m_in, l_in
    else:
        acc_ref, m_ref, l_ref, k_buf, v_buf, lane_ref = rest
    index = info[0]
    rows = q_buf.shape[0]
    tokens = rows // heads
    size = TILE * heads
    core = index % 2
    distance = jnp.where(index // 2 % 2 == 0, distances[0], distances[1])
    base = (index - core - 2 * distance) * tokens
    end = jnp.where(distance > 0, base + 2 * tokens, -1)

    @pl.when(low_ref[0] < end)
    def _():
        fill_lanes(lane_ref)
        place(mine_ref, core * tokens, k_buf, v_buf)
        place(other_ref, (1 - core) * tokens, k_buf, v_buf)

        def tile_body(tile, carry):
            skip = low_ref[tile] - base
            for begin in range(0, 2 * tokens, WINDOW):
                reached = skip < begin + WINDOW
                if begin:
                    reached &= skip >= begin

                @pl.when(reached)
                def _():
                    for _, at in chunks(tile, size):
                        step(at, q_buf[at, :], (begin, 2 * tokens), None, base, k_buf, v_buf, lane_ref, qs_ref, acc_ref, m_ref, l_ref)

            return carry

        lax.fori_loop(0, rows // size, tile_body, 0)

    if last:
        copies = []
        for part in range(rows // CHUNK):
            at = slice(part * CHUNK, (part + 1) * CHUNK)
            out_ref[at, :] = acc_ref[at, :] / jnp.sum(l_ref[at, :], axis=1, keepdims=True)
            copies.append(pltpu.make_async_copy(out_ref.at[at], out_hbm.at[at], sems.at[part]))
            copies[-1].start()
        for copy in copies:
            copy.wait()


VMEM = pl.BlockSpec(memory_space=pltpu.VMEM)
SMEM = pl.BlockSpec(memory_space=pltpu.SMEM)
HBM = pl.BlockSpec(memory_space=pltpu.HBM)
LIMIT = 24 << 20


def buffers(tokens):
    split = pltpu.VMEM((2 * tokens, 256), BF16)
    return [split, split, pltpu.VMEM((8, 2 * tokens), jnp.int32)]


def attend_own(heads, info, lens, q, mine, other):
    rows = q.shape[0]
    tokens = rows // heads
    full = jax.ShapeDtypeStruct((rows, 128), F32)
    return pl.pallas_call(
        functools.partial(own_kernel, heads),
        name="own_pair",
        out_shape=(
            full,
            full,
            full,
            jax.ShapeDtypeStruct((rows, 256), BF16),
            jax.ShapeDtypeStruct((rows, 128), jnp.int32),
            jax.ShapeDtypeStruct((rows // (TILE * heads),), jnp.int32),
        ),
        in_specs=[SMEM, HBM, HBM, VMEM, VMEM],
        out_specs=(VMEM, VMEM, VMEM, VMEM, VMEM, SMEM),
        scratch_shapes=buffers(tokens)
        + [pltpu.VMEM((rows, 128), F32), pltpu.VMEM(lens.shape, jnp.int32), pltpu.SemaphoreType.DMA((2,))],
        compiler_params=pltpu.CompilerParams(vmem_limit_bytes=LIMIT),
    )(info, lens, q, mine, other)


def attend_back(heads, distances, last, info, low, q_buf, qs, state, pieces):
    rows = q_buf.shape[0]
    tokens = rows // heads
    full = jax.ShapeDtypeStruct((rows, 128), F32)
    tail = [pltpu.VMEM((rows, 128), F32), pltpu.SemaphoreType.DMA((rows // CHUNK,))]
    return pl.pallas_call(
        functools.partial(back_kernel, heads, distances, last),
        out_shape=full if last else (full, full, full),
        in_specs=[SMEM, SMEM] + [VMEM] * 7,
        out_specs=HBM if last else (VMEM, VMEM, VMEM),
        input_output_aliases={} if last else {4: 0, 5: 1, 6: 2},
        scratch_shapes=buffers(tokens) + (tail if last else []),
        compiler_params=pltpu.CompilerParams(vmem_limit_bytes=LIMIT),
    )(info, low, q_buf, qs, *state, *pieces)


def attend(queries, key_rows, value_rows, doc_lengths):
    tokens, heads, width = queries.shape
    count = lax.axis_size(AXES)
    index = lax.axis_index(AXES).astype(jnp.int32)
    info = jnp.reshape(index, (1,))
    q = pltpu.with_memory_space_constraint(queries.reshape(tokens * heads, width), pltpu.HBM)
    lens = pltpu.with_memory_space_constraint(doc_lengths.reshape(1, -1), pltpu.HBM)
    devices = range(count)
    even = [i for i in devices if i // 2 % 2 == 0]
    odd = [i for i in devices if i // 2 % 2 == 1]

    def send(x, pairs):
        return lax.ppermute(x, AXES, pairs)

    def swap(x, among=devices):
        return send(x, [(i, i ^ 1) for i in among])

    def after(x, state):
        x, *state = lax.optimization_barrier((x, *state))
        return x, state

    up = [(i, i + 4) for i in devices if i + 4 < count]
    held = jnp.stack([key_rows, value_rows]).reshape(2 * tokens, width)
    held_other = swap(held)
    up_1 = send(held, up)
    across_1 = send(held, [(i, i + 2) for i in even])
    *state, q_buf, qs, low = attend_own(heads, info, lens, q, held, held_other)

    def back(distances, last, pieces, state):
        return attend_back(heads, distances, last, info, low, q_buf, qs, state, pieces)

    up_1, state = after(up_1, state)
    up_2 = send(up_1, up)
    across_2 = send(up_1, [(i, i ^ 2) for i in devices])
    state = back((2, 2), False, (up_1, swap(up_1)), state)
    across_1, state = after(across_1, state)
    state = back((0, 1), False, (across_1, swap(across_1, odd)), state)
    up_2, state = after(up_2, state)
    across_2, state = after(across_2, state)
    across_3 = send(up_2, [(i, i - 2) for i in odd])
    up_2_other = swap(up_2)
    across_2_other = swap(across_2)
    state = back((4, 4), False, (up_2, up_2_other), state)
    state = back((1, 3), False, (across_2, across_2_other), state)
    across_3, state = after(across_3, state)
    out = back((3, 0), True, (across_3, swap(across_3, even)), state)
    return out.reshape(tokens, heads, width)


def solution(mesh):
    in_specs = (P(AXES, None, None), P(AXES, None), P(AXES, None), P())
    return jax.shard_map(attend, mesh=mesh, in_specs=in_specs, out_specs=P(AXES, None, None), check_vma=False)
```

```python
import functools
import math

import jax
import jax.numpy as jnp
from jax import lax
from jax.experimental import pallas as pl
from jax.experimental.pallas import tpu as pltpu
from jax.sharding import PartitionSpec as P

AXES = ("inner", "outer")
NEGATIVE = -1e30
TILE = 192
TRIMS = (0, 256, 512)
CHUNK = 256
BF16 = jnp.bfloat16
F32 = jnp.float32


def halves(x):
    high = x.astype(BF16)
    return high, (x - high.astype(F32)).astype(BF16)


def place(kv_ref, start, k_buf, v_buf):
    rows = kv_ref.shape[0] // 2
    at = pl.ds(pl.multiple_of(start, 128), rows)
    for source, target in ((kv_ref[0:rows, :], k_buf), (kv_ref[rows : 2 * rows, :], v_buf)):
        high, low = halves(source)
        target[at, 0:128] = high
        target[at, 128:256] = low


def fill_lanes(lane_ref):
    lane_ref[...] = lax.broadcasted_iota(jnp.int32, lane_ref.shape, 1)


def spread(ref, lanes, rows):
    x = ref[0:8, lanes]
    return jnp.broadcast_to(x[None], (rows // 8,) + x.shape).reshape(rows, x.shape[1])


def step(rows, q_all, window, row_pos, base, k_buf, v_buf, lane_ref, qs_ref, acc_ref, m_ref, l_ref):
    first = row_pos is not None
    keys = slice(*window)
    nt = (((1,), (1,)), ((), ()))
    k_high = k_buf[keys, 0:128]
    scores = lax.dot_general(q_all, jnp.concatenate([k_high, k_high], axis=1), nt, preferred_element_type=F32)
    scores += lax.dot_general(q_all[:, 0:128], k_buf[keys, 128:256], nt, preferred_element_type=F32)
    low = qs_ref[rows, :] - base
    if first:
        low = low - jnp.int32(-(2**31))
        bound = row_pos - base - low
    parts = []
    for c in range((window[1] - window[0]) // 128):
        s = scores[:, c * 128 : (c + 1) * 128]
        lane = spread(lane_ref, slice(window[0] + c * 128, window[0] + (c + 1) * 128), s.shape[0])
        allowed = lane - low <= bound if first else lane >= low
        parts.append(jnp.where(allowed, s, NEGATIVE))
    top = functools.reduce(jnp.maximum, parts)
    top = jnp.broadcast_to(jnp.max(top, axis=1, keepdims=True), top.shape)
    if not first:
        before = m_ref[rows, :]
        top = jnp.maximum(before, top)
        shrink = jnp.exp2(before - top)
    highs, lows, total = [], [], None
    for s in parts:
        p = jnp.exp2(s - top)
        total = p if total is None else total + p
        high, rest = halves(p)
        highs.append(high)
        lows.append(rest)
    values = v_buf[keys, :]
    values = jnp.concatenate([values, values], axis=0)
    mixed = jnp.dot(jnp.concatenate(highs + lows, axis=1), values, preferred_element_type=F32)
    mixed = mixed[:, 0:128] + mixed[:, 128:256]
    if first:
        l_ref[rows, :] = total
        acc_ref[rows, :] = mixed
    else:
        l_ref[rows, :] = l_ref[rows, :] * shrink + total
        acc_ref[rows, :] = acc_ref[rows, :] * shrink + mixed
    m_ref[rows, :] = top


def chunks(tile, size):
    for part in range(size // CHUNK):
        begin = tile * size + part * CHUNK
        yield begin, pl.ds(pl.multiple_of(begin, CHUNK), CHUNK)


def own_kernel(heads, info, lens_hbm, q_hbm, mine_ref, other_ref, acc_ref, m_ref, l_ref, q_buf, qs_ref, low_ref, *scratch):
    k_buf, v_buf, lane_ref, q_ref, lens_ref, sems = scratch
    fetch_lens = pltpu.make_async_copy(lens_hbm, lens_ref, sems.at[0])
    fetch_lens.start()
    fetch = pltpu.make_async_copy(q_hbm, q_ref, sems.at[1])
    fetch.start()
    index = info[0]
    rows = q_ref.shape[0]
    tokens = rows // heads
    core = index % 2
    base = (index - core) * tokens
    place(mine_ref, core * tokens, k_buf, v_buf)
    place(other_ref, (1 - core) * tokens, k_buf, v_buf)
    fetch_lens.wait()
    docs = lens_ref.shape[1]
    lens = jnp.broadcast_to(lens_ref[...], (8, docs))
    ahead = lax.broadcasted_iota(jnp.int32, (docs, docs), 0) < lax.broadcasted_iota(jnp.int32, (docs, docs), 1)
    ahead = ahead.astype(F32).astype(BF16)
    coarse = jnp.dot((lens // 64).astype(F32).astype(BF16), ahead, preferred_element_type=F32)
    fine = jnp.dot((lens % 64).astype(F32).astype(BF16), ahead, preferred_element_type=F32)
    starts = (coarse * 64.0 + fine)[0:1, :]
    pos = lax.broadcasted_iota(jnp.int32, (tokens, docs), 0) + index * tokens
    begun = jnp.where(starts <= pos.astype(F32), jnp.broadcast_to(starts, pos.shape), 0.0)
    start = jnp.max(begun, axis=1, keepdims=True).astype(jnp.int32)
    start = jnp.broadcast_to(jnp.broadcast_to(start, (tokens, 128))[:, None, :], (tokens, heads, 128))
    qs_ref[...] = start.reshape(rows, 128)
    fill_lanes(lane_ref)
    size = TILE * heads
    for tile in range(rows // size):
        low_ref[tile] = jnp.max(qs_ref[tile * size : tile * size + 8, :])
    fetch.wait()
    short = 512

    def tile_body(tile, carry):
        def attend(window):
            for begin, at in chunks(tile, size):
                high, low = halves(q_ref[at, :] * (math.log2(math.e) / math.sqrt(q_ref.shape[1])))
                q_all = jnp.concatenate([high, low], axis=1)
                q_buf[at, :] = q_all
                row = lax.broadcasted_iota(jnp.int32, (CHUNK, 128), 0) + begin
                step(at, q_all, window, index * tokens + row // heads, base, k_buf, v_buf, lane_ref, qs_ref, acc_ref, m_ref, l_ref)

        fits = core * tokens + (tile + 1) * TILE <= short
        pl.when(fits)(lambda: attend((0, short)))
        pl.when(jnp.logical_not(fits))(lambda: attend((0, 2 * tokens)))
        return carry

    lax.fori_loop(0, rows // size, tile_body, 0)


def back_kernel(heads, units, trims, last, info, low_ref, q_buf, qs_ref, acc_in, m_in, l_in, *rest):
    pieces, rest = rest[: 2 * len(units)], rest[2 * len(units) :]
    if last:
        out_hbm, k_buf, v_buf, lane_ref, out_ref, sems = rest
        acc_ref, m_ref, l_ref = acc_in, m_in, l_in
    else:
        acc_ref, m_ref, l_ref, k_buf, v_buf, lane_ref = rest
    index = info[0]
    rows = q_buf.shape[0]
    tokens = rows // heads
    size = TILE * heads
    core = index % 2
    fill_lanes(lane_ref)

    def out_copy(tile):
        at = pl.ds(pl.multiple_of(tile * size, size), size)
        return pltpu.make_async_copy(out_ref.at[at], out_hbm.at[at], sems.at[tile])

    def unit_body(n, carry):
        distance = jnp.int32(0)
        for m, pair in enumerate(units):
            distance = jnp.where(n == m, jnp.where(index // 2 % 2 == 0, pair[0], pair[1]), distance)
        base = (index - core - 2 * distance) * tokens
        end = jnp.where(distance > 0, base + 2 * tokens, -1)
        for m in range(len(units)):

            @pl.when((n == m) & (low_ref[0] < end))
            def _():
                place(pieces[2 * m], core * tokens, k_buf, v_buf)
                place(pieces[2 * m + 1], (1 - core) * tokens, k_buf, v_buf)

        def tile_body(tile, carry):
            skip = low_ref[tile] - base
            for begin, stop in zip(trims, trims[1:] + (2 * tokens,)):
                reached = (skip < stop) & (low_ref[tile] < end)
                if begin:
                    reached &= skip >= begin

                @pl.when(reached)
                def _():
                    for _, at in chunks(tile, size):
                        step(at, q_buf[at, :], (begin, 2 * tokens), None, base, k_buf, v_buf, lane_ref, qs_ref, acc_ref, m_ref, l_ref)

            if last:
                for _, at in chunks(tile, size):
                    out_ref[at, :] = acc_ref[at, :] / jnp.sum(l_ref[at, :], axis=1, keepdims=True)
                out_copy(tile).start()
            return carry

        lax.fori_loop(0, rows // size, tile_body, 0)
        return carry

    if len(units) == 1:
        unit_body(0, 0)
    else:
        lax.fori_loop(0, len(units), unit_body, 0)
    if last:
        for tile in range(rows // size):
            out_copy(tile).wait()


VMEM = pl.BlockSpec(memory_space=pltpu.VMEM)
SMEM = pl.BlockSpec(memory_space=pltpu.SMEM)
HBM = pl.BlockSpec(memory_space=pltpu.HBM)
LIMIT = 24 << 20


def buffers(tokens):
    split = pltpu.VMEM((2 * tokens, 256), BF16)
    return [split, split, pltpu.VMEM((8, 2 * tokens), jnp.int32)]


def attend_own(heads, info, lens, q, mine, other):
    rows = q.shape[0]
    tokens = rows // heads
    full = jax.ShapeDtypeStruct((rows, 128), F32)
    return pl.pallas_call(
        functools.partial(own_kernel, heads),
        name="own_pair",
        out_shape=(
            full,
            full,
            full,
            jax.ShapeDtypeStruct((rows, 256), BF16),
            jax.ShapeDtypeStruct((rows, 128), jnp.int32),
            jax.ShapeDtypeStruct((rows // (TILE * heads),), jnp.int32),
        ),
        in_specs=[SMEM, HBM, HBM, VMEM, VMEM],
        out_specs=(VMEM, VMEM, VMEM, VMEM, VMEM, SMEM),
        scratch_shapes=buffers(tokens)
        + [pltpu.VMEM((rows, 128), F32), pltpu.VMEM(lens.shape, jnp.int32), pltpu.SemaphoreType.DMA((2,))],
        compiler_params=pltpu.CompilerParams(vmem_limit_bytes=LIMIT),
    )(info, lens, q, mine, other)


def attend_back(heads, units, trims, last, info, low, q_buf, qs, state, pieces):
    rows = q_buf.shape[0]
    tokens = rows // heads
    full = jax.ShapeDtypeStruct((rows, 128), F32)
    tail = [pltpu.VMEM((rows, 128), F32), pltpu.SemaphoreType.DMA((rows // (TILE * heads),))]
    return pl.pallas_call(
        functools.partial(back_kernel, heads, units, trims, last),
        out_shape=full if last else (full, full, full),
        in_specs=[SMEM, SMEM] + [VMEM] * (5 + len(pieces)),
        out_specs=HBM if last else (VMEM, VMEM, VMEM),
        input_output_aliases={} if last else {4: 0, 5: 1, 6: 2},
        scratch_shapes=buffers(tokens) + (tail if last else []),
        compiler_params=pltpu.CompilerParams(vmem_limit_bytes=LIMIT),
    )(info, low, q_buf, qs, *state, *pieces)


def attend(queries, key_rows, value_rows, doc_lengths):
    tokens, heads, width = queries.shape
    count = lax.axis_size(AXES)
    index = lax.axis_index(AXES).astype(jnp.int32)
    info = jnp.reshape(index, (1,))
    q = pltpu.with_memory_space_constraint(queries.reshape(tokens * heads, width), pltpu.HBM)
    lens = pltpu.with_memory_space_constraint(doc_lengths.reshape(1, -1), pltpu.HBM)
    devices = range(count)
    even = [i for i in devices if i // 2 % 2 == 0]
    odd = [i for i in devices if i // 2 % 2 == 1]

    def send(x, pairs):
        return lax.ppermute(x, AXES, pairs)

    def swap(x, among=devices):
        return send(x, [(i, i ^ 1) for i in among])

    def after(x, state):
        x, *state = lax.optimization_barrier((x, *state))
        return x, state

    up = [(i, i + 4) for i in devices if i + 4 < count]
    held = jnp.stack([key_rows, value_rows]).reshape(2 * tokens, width)
    held_other = swap(held)
    up_1 = send(held, up)
    across_1 = send(held, [(i, i + 2) for i in even])
    *state, q_buf, qs, low = attend_own(heads, info, lens, q, held, held_other)

    def back(units, trims, last, pieces, state):
        return attend_back(heads, units, trims, last, info, low, q_buf, qs, state, pieces)

    up_1, state = after(up_1, state)
    up_2 = send(up_1, up)
    across_2 = send(up_1, [(i, i ^ 2) for i in devices])
    state = back(((2, 2),), (0,), False, (up_1, swap(up_1)), state)
    across_1, state = after(across_1, state)
    state = back(((0, 1),), (0,), False, (across_1, swap(across_1, odd)), state)
    up_2, state = after(up_2, state)
    across_2, state = after(across_2, state)
    across_3 = send(up_2, [(i, i - 2) for i in odd])
    pieces = (up_2, swap(up_2), across_2, swap(across_2))
    state = back(((4, 4), (1, 3)), TRIMS, False, pieces, state)
    across_3, state = after(across_3, state)
    out = back(((3, 0),), TRIMS, True, (across_3, swap(across_3, even)), state)
    return out.reshape(tokens, heads, width)


def solution(mesh):
    in_specs = (P(AXES, None, None), P(AXES, None), P(AXES, None), P())
    return jax.shard_map(attend, mesh=mesh, in_specs=in_specs, out_specs=P(AXES, None, None), check_vma=False)
```

```python
import functools
import math

import jax
import jax.numpy as jnp
from jax import lax
from jax.experimental import pallas as pl
from jax.experimental.pallas import tpu as pltpu
from jax.sharding import PartitionSpec as P

AXES = ("inner", "outer")
NEGATIVE = -1e30
TILE = 192
TRIMS = (0, 256, 512)
CHUNK = 256
BF16 = jnp.bfloat16
F32 = jnp.float32


def halves(x):
    high = x.astype(BF16)
    return high, (x - high.astype(F32)).astype(BF16)


def place(kv_ref, start, k_buf, v_buf):
    rows = kv_ref.shape[0] // 2
    at = pl.ds(pl.multiple_of(start, 128), rows)
    for source, target in ((kv_ref[0:rows, :], k_buf), (kv_ref[rows : 2 * rows, :], v_buf)):
        high, low = halves(source)
        target[at, 0:128] = high
        target[at, 128:256] = low


def fill_lanes(lane_ref):
    lane_ref[...] = lax.broadcasted_iota(jnp.int32, lane_ref.shape, 1)


def spread(ref, lanes, rows):
    x = ref[0:8, lanes]
    return jnp.broadcast_to(x[None], (rows // 8,) + x.shape).reshape(rows, x.shape[1])


def step(rows, q_all, window, row_pos, base, k_buf, v_buf, lane_ref, qs_ref, acc_ref, m_ref, l_ref):
    first = row_pos is not None
    keys = slice(*window)
    nt = (((1,), (1,)), ((), ()))
    k_high = k_buf[keys, 0:128]
    scores = lax.dot_general(q_all, jnp.concatenate([k_high, k_high], axis=1), nt, preferred_element_type=F32)
    scores += lax.dot_general(q_all[:, 0:128], k_buf[keys, 128:256], nt, preferred_element_type=F32)
    low = qs_ref[rows, :] - base
    if first:
        low = low - jnp.int32(-(2**31))
        bound = row_pos - base - low
    parts = []
    for c in range((window[1] - window[0]) // 128):
        s = scores[:, c * 128 : (c + 1) * 128]
        lane = spread(lane_ref, slice(window[0] + c * 128, window[0] + (c + 1) * 128), s.shape[0])
        allowed = lane - low <= bound if first else lane >= low
        parts.append(jnp.where(allowed, s, NEGATIVE))
    top = functools.reduce(jnp.maximum, parts)
    top = jnp.broadcast_to(jnp.max(top, axis=1, keepdims=True), top.shape)
    if not first:
        before = m_ref[rows, :]
        top = jnp.maximum(before, top)
        shrink = jnp.exp2(before - top)
    highs, lows, total = [], [], None
    for s in parts:
        p = jnp.exp2(s - top)
        total = p if total is None else total + p
        high, rest = halves(p)
        highs.append(high)
        lows.append(rest)
    values = v_buf[keys, :]
    values = jnp.concatenate([values, values], axis=0)
    mixed = jnp.dot(jnp.concatenate(highs + lows, axis=1), values, preferred_element_type=F32)
    mixed = mixed[:, 0:128] + mixed[:, 128:256]
    if first:
        l_ref[rows, :] = total
        acc_ref[rows, :] = mixed
    else:
        l_ref[rows, :] = l_ref[rows, :] * shrink + total
        acc_ref[rows, :] = acc_ref[rows, :] * shrink + mixed
    m_ref[rows, :] = top


def chunks(tile, size):
    for part in range(size // CHUNK):
        begin = tile * size + part * CHUNK
        yield begin, pl.ds(pl.multiple_of(begin, CHUNK), CHUNK)


def own_kernel(heads, info, lens_hbm, q_hbm, mine_ref, other_ref, acc_ref, m_ref, l_ref, q_buf, qs_ref, low_ref, *scratch):
    k_buf, v_buf, lane_ref, q_ref, lens_ref, sems = scratch
    fetch_lens = pltpu.make_async_copy(lens_hbm, lens_ref, sems.at[0])
    fetch_lens.start()
    fetch = pltpu.make_async_copy(q_hbm, q_ref, sems.at[1])
    fetch.start()
    index = info[0]
    rows = q_ref.shape[0]
    tokens = rows // heads
    core = index % 2
    base = (index - core) * tokens
    place(mine_ref, core * tokens, k_buf, v_buf)
    place(other_ref, (1 - core) * tokens, k_buf, v_buf)
    fetch_lens.wait()
    docs = lens_ref.shape[1]
    lens = jnp.broadcast_to(lens_ref[...], (8, docs))
    ahead = lax.broadcasted_iota(jnp.int32, (docs, docs), 0) < lax.broadcasted_iota(jnp.int32, (docs, docs), 1)
    ahead = ahead.astype(F32).astype(BF16)
    coarse = jnp.dot((lens // 64).astype(F32).astype(BF16), ahead, preferred_element_type=F32)
    fine = jnp.dot((lens % 64).astype(F32).astype(BF16), ahead, preferred_element_type=F32)
    starts = (coarse * 64.0 + fine)[0:1, :]
    pos = lax.broadcasted_iota(jnp.int32, (tokens, docs), 0) + index * tokens
    begun = jnp.where(starts <= pos.astype(F32), jnp.broadcast_to(starts, pos.shape), 0.0)
    start = jnp.max(begun, axis=1, keepdims=True).astype(jnp.int32)
    start = jnp.broadcast_to(jnp.broadcast_to(start, (tokens, 128))[:, None, :], (tokens, heads, 128))
    qs_ref[...] = start.reshape(rows, 128)
    fill_lanes(lane_ref)
    size = TILE * heads
    for tile in range(rows // size):
        low_ref[tile] = jnp.max(qs_ref[tile * size : tile * size + 8, :])
    fetch.wait()
    short = 512

    def tile_body(tile, carry):
        def attend(window):
            for begin, at in chunks(tile, size):
                high, low = halves(q_ref[at, :] * (math.log2(math.e) / math.sqrt(q_ref.shape[1])))
                q_all = jnp.concatenate([high, low], axis=1)
                q_buf[at, :] = q_all
                row = lax.broadcasted_iota(jnp.int32, (CHUNK, 128), 0) + begin
                step(at, q_all, window, index * tokens + row // heads, base, k_buf, v_buf, lane_ref, qs_ref, acc_ref, m_ref, l_ref)

        fits = core * tokens + (tile + 1) * TILE <= short
        pl.when(fits)(lambda: attend((0, short)))
        pl.when(jnp.logical_not(fits))(lambda: attend((0, 2 * tokens)))
        return carry

    lax.fori_loop(0, rows // size, tile_body, 0)


def back_kernel(heads, units, trims, last, info, low_ref, q_buf, qs_ref, acc_in, m_in, l_in, *rest):
    pieces, rest = rest[: 2 * len(units)], rest[2 * len(units) :]
    if last:
        out_hbm, k_buf, v_buf, lane_ref, out_ref, sems = rest
        acc_ref, m_ref, l_ref = acc_in, m_in, l_in
    else:
        acc_ref, m_ref, l_ref, k_buf, v_buf, lane_ref = rest
    index = info[0]
    rows = q_buf.shape[0]
    tokens = rows // heads
    size = TILE * heads
    core = index % 2
    fill_lanes(lane_ref)

    def out_copy(tile):
        at = pl.ds(pl.multiple_of(tile * size, size), size)
        return pltpu.make_async_copy(out_ref.at[at], out_hbm.at[at], sems.at[tile])

    def unit_body(n, carry):
        distance = jnp.int32(0)
        for m, pair in enumerate(units):
            distance = jnp.where(n == m, jnp.where(index // 2 % 2 == 0, pair[0], pair[1]), distance)
        base = (index - core - 2 * distance) * tokens
        end = jnp.where(distance > 0, base + 2 * tokens, -1)
        for m in range(len(units)):

            @pl.when((n == m) & (low_ref[0] < end))
            def _():
                place(pieces[2 * m], core * tokens, k_buf, v_buf)
                place(pieces[2 * m + 1], (1 - core) * tokens, k_buf, v_buf)

        def tile_body(tile, carry):
            skip = low_ref[tile] - base
            for begin, stop in zip(trims, trims[1:] + (2 * tokens,)):
                reached = (skip < stop) & (low_ref[tile] < end)
                if begin:
                    reached &= skip >= begin

                @pl.when(reached)
                def _():
                    for _, at in chunks(tile, size):
                        step(at, q_buf[at, :], (begin, 2 * tokens), None, base, k_buf, v_buf, lane_ref, qs_ref, acc_ref, m_ref, l_ref)

            if last:
                for _, at in chunks(tile, size):
                    out_ref[at, :] = acc_ref[at, :] / jnp.sum(l_ref[at, :], axis=1, keepdims=True)
                out_copy(tile).start()
            return carry

        lax.fori_loop(0, rows // size, tile_body, 0)
        return carry

    if len(units) == 1:
        unit_body(0, 0)
    else:
        lax.fori_loop(0, len(units), unit_body, 0)
    if last:
        for tile in range(rows // size):
            out_copy(tile).wait()


VMEM = pl.BlockSpec(memory_space=pltpu.VMEM)
SMEM = pl.BlockSpec(memory_space=pltpu.SMEM)
HBM = pl.BlockSpec(memory_space=pltpu.HBM)
LIMIT = 24 << 20


def buffers(tokens):
    split = pltpu.VMEM((2 * tokens, 256), BF16)
    return [split, split, pltpu.VMEM((8, 2 * tokens), jnp.int32)]


def attend_own(heads, info, lens, q, mine, other):
    rows = q.shape[0]
    tokens = rows // heads
    full = jax.ShapeDtypeStruct((rows, 128), F32)
    return pl.pallas_call(
        functools.partial(own_kernel, heads),
        name="own_pair",
        out_shape=(
            full,
            full,
            full,
            jax.ShapeDtypeStruct((rows, 256), BF16),
            jax.ShapeDtypeStruct((rows, 128), jnp.int32),
            jax.ShapeDtypeStruct((rows // (TILE * heads),), jnp.int32),
        ),
        in_specs=[SMEM, HBM, HBM, VMEM, VMEM],
        out_specs=(VMEM, VMEM, VMEM, VMEM, VMEM, SMEM),
        scratch_shapes=buffers(tokens)
        + [pltpu.VMEM((rows, 128), F32), pltpu.VMEM(lens.shape, jnp.int32), pltpu.SemaphoreType.DMA((2,))],
        compiler_params=pltpu.CompilerParams(vmem_limit_bytes=LIMIT),
    )(info, lens, q, mine, other)


def attend_back(heads, units, trims, last, info, low, q_buf, qs, state, pieces):
    rows = q_buf.shape[0]
    tokens = rows // heads
    full = jax.ShapeDtypeStruct((rows, 128), F32)
    tail = [pltpu.VMEM((rows, 128), F32), pltpu.SemaphoreType.DMA((rows // (TILE * heads),))]
    return pl.pallas_call(
        functools.partial(back_kernel, heads, units, trims, last),
        out_shape=full if last else (full, full, full),
        in_specs=[SMEM, SMEM] + [VMEM] * (5 + len(pieces)),
        out_specs=HBM if last else (VMEM, VMEM, VMEM),
        input_output_aliases={} if last else {4: 0, 5: 1, 6: 2},
        scratch_shapes=buffers(tokens) + (tail if last else []),
        compiler_params=pltpu.CompilerParams(vmem_limit_bytes=LIMIT),
    )(info, low, q_buf, qs, *state, *pieces)


def attend(queries, key_rows, value_rows, doc_lengths):
    tokens, heads, width = queries.shape
    count = lax.axis_size(AXES)
    index = lax.axis_index(AXES).astype(jnp.int32)
    info = jnp.reshape(index, (1,))
    q = pltpu.with_memory_space_constraint(queries.reshape(tokens * heads, width), pltpu.HBM)
    lens = pltpu.with_memory_space_constraint(doc_lengths.reshape(1, -1), pltpu.HBM)
    devices = range(count)
    even = [i for i in devices if i // 2 % 2 == 0]
    odd = [i for i in devices if i // 2 % 2 == 1]

    def send(x, pairs):
        return lax.ppermute(x, AXES, pairs)

    def swap(x, among=devices):
        return send(x, [(i, i ^ 1) for i in among])

    def after(x, state):
        x, *state = lax.optimization_barrier((x, *state))
        return x, state

    up = [(i, i + 4) for i in devices if i + 4 < count]
    held = jnp.stack([key_rows, value_rows]).reshape(2 * tokens, width)
    held_other = swap(held)
    up_1 = send(held, up)
    across_1 = send(held, [(i, i + 2) for i in even])
    *state, q_buf, qs, low = attend_own(heads, info, lens, q, held, held_other)

    def back(units, trims, last, pieces, state):
        return attend_back(heads, units, trims, last, info, low, q_buf, qs, state, pieces)

    up_1, state = after(up_1, state)
    up_2 = send(up_1, up)
    across_2 = send(up_1, [(i, i ^ 2) for i in devices])
    up_1_other = swap(up_1)
    across_1, state = after(across_1, state)
    across_1_other = swap(across_1, odd)
    state = back(((2, 2),), (0,), False, (up_1, up_1_other), state)
    up_2, state = after(up_2, state)
    across_3 = send(up_2, [(i, i - 2) for i in odd])
    up_2_other = swap(up_2)
    state = back(((0, 1),), (0,), False, (across_1, across_1_other), state)
    across_2, state = after(across_2, state)
    pieces = (up_2, up_2_other, across_2, swap(across_2))
    state = back(((4, 4), (1, 3)), TRIMS, False, pieces, state)
    across_3, state = after(across_3, state)
    out = back(((3, 0),), TRIMS, True, (across_3, swap(across_3, even)), state)
    return out.reshape(tokens, heads, width)


def solution(mesh):
    in_specs = (P(AXES, None, None), P(AXES, None), P(AXES, None), P())
    return jax.shard_map(attend, mesh=mesh, in_specs=in_specs, out_specs=P(AXES, None, None), check_vma=False)
```

```python
import functools
import math

import jax
import jax.numpy as jnp
from jax import lax
from jax.experimental import pallas as pl
from jax.experimental.pallas import tpu as pltpu
from jax.sharding import PartitionSpec as P

AXES = ("inner", "outer")
NEGATIVE = -1e30
TILE = 192
TRIMS = (0, 256, 512)
CHUNK = 256
BF16 = jnp.bfloat16
F32 = jnp.float32


def halves(x):
    high = x.astype(BF16)
    return high, (x - high.astype(F32)).astype(BF16)


def place(kv_ref, start, k_buf, v_buf):
    rows = kv_ref.shape[0] // 2
    at = pl.ds(pl.multiple_of(start, 128), rows)
    for source, target in ((kv_ref[0:rows, :], k_buf), (kv_ref[rows : 2 * rows, :], v_buf)):
        high, low = halves(source)
        target[at, 0:128] = high
        target[at, 128:256] = low


def fill_lanes(lane_ref):
    lane_ref[...] = lax.broadcasted_iota(jnp.int32, lane_ref.shape, 1)


def spread(ref, lanes, rows):
    x = ref[0:8, lanes]
    return jnp.broadcast_to(x[None], (rows // 8,) + x.shape).reshape(rows, x.shape[1])


def step(rows, q_all, window, row_pos, base, k_buf, v_buf, lane_ref, qs_ref, acc_ref, m_ref, l_ref):
    first = row_pos is not None
    keys = slice(*window)
    nt = (((1,), (1,)), ((), ()))
    k_high = k_buf[keys, 0:128]
    scores = lax.dot_general(q_all, jnp.concatenate([k_high, k_high], axis=1), nt, preferred_element_type=F32)
    scores += lax.dot_general(q_all[:, 0:128], k_buf[keys, 128:256], nt, preferred_element_type=F32)
    low = qs_ref[rows, :] - base
    if first:
        low = low - jnp.int32(-(2**31))
        bound = row_pos - base - low
    parts = []
    for c in range((window[1] - window[0]) // 128):
        s = scores[:, c * 128 : (c + 1) * 128]
        lane = spread(lane_ref, slice(window[0] + c * 128, window[0] + (c + 1) * 128), s.shape[0])
        allowed = lane - low <= bound if first else lane >= low
        parts.append(jnp.where(allowed, s, NEGATIVE))
    top = functools.reduce(jnp.maximum, parts)
    top = jnp.broadcast_to(jnp.max(top, axis=1, keepdims=True), top.shape)
    if not first:
        before = m_ref[rows, :]
        top = jnp.maximum(before, top)
        shrink = jnp.exp2(before - top)
    highs, lows, total = [], [], None
    for s in parts:
        p = jnp.exp2(s - top)
        total = p if total is None else total + p
        high, rest = halves(p)
        highs.append(high)
        lows.append(rest)
    values = v_buf[keys, :]
    values = jnp.concatenate([values, values], axis=0)
    mixed = jnp.dot(jnp.concatenate(highs + lows, axis=1), values, preferred_element_type=F32)
    mixed = mixed[:, 0:128] + mixed[:, 128:256]
    if first:
        l_ref[rows, :] = total
        acc_ref[rows, :] = mixed
    else:
        l_ref[rows, :] = l_ref[rows, :] * shrink + total
        acc_ref[rows, :] = acc_ref[rows, :] * shrink + mixed
    m_ref[rows, :] = top


def chunks(tile, size):
    for part in range(size // CHUNK):
        begin = tile * size + part * CHUNK
        yield begin, pl.ds(pl.multiple_of(begin, CHUNK), CHUNK)


def own_kernel(heads, info, lens_hbm, q_hbm, mine_ref, other_ref, acc_ref, m_ref, l_ref, q_buf, qs_ref, low_ref, *scratch):
    k_buf, v_buf, lane_ref, q_ref, lens_ref, sems = scratch
    fetch_lens = pltpu.make_async_copy(lens_hbm, lens_ref, sems.at[0])
    fetch_lens.start()
    fetch = pltpu.make_async_copy(q_hbm, q_ref, sems.at[1])
    fetch.start()
    index = info[0]
    rows = q_ref.shape[0]
    tokens = rows // heads
    core = index % 2
    base = (index - core) * tokens
    place(mine_ref, core * tokens, k_buf, v_buf)
    place(other_ref, (1 - core) * tokens, k_buf, v_buf)
    fetch_lens.wait()
    docs = lens_ref.shape[1]
    lens = jnp.broadcast_to(lens_ref[...], (8, docs))
    ahead = lax.broadcasted_iota(jnp.int32, (docs, docs), 0) < lax.broadcasted_iota(jnp.int32, (docs, docs), 1)
    ahead = ahead.astype(F32).astype(BF16)
    coarse = jnp.dot((lens // 64).astype(F32).astype(BF16), ahead, preferred_element_type=F32)
    fine = jnp.dot((lens % 64).astype(F32).astype(BF16), ahead, preferred_element_type=F32)
    starts = (coarse * 64.0 + fine)[0:1, :]
    pos = lax.broadcasted_iota(jnp.int32, (tokens, docs), 0) + index * tokens
    begun = jnp.where(starts <= pos.astype(F32), jnp.broadcast_to(starts, pos.shape), 0.0)
    start = jnp.max(begun, axis=1, keepdims=True).astype(jnp.int32)
    start = jnp.broadcast_to(jnp.broadcast_to(start, (tokens, 128))[:, None, :], (tokens, heads, 128))
    qs_ref[...] = start.reshape(rows, 128)
    fill_lanes(lane_ref)
    size = TILE * heads
    for tile in range(rows // size):
        low_ref[tile] = jnp.max(qs_ref[tile * size : tile * size + 8, :])
    fetch.wait()
    short = 512

    def tile_body(tile, carry):
        def attend(window):
            for begin, at in chunks(tile, size):
                high, low = halves(q_ref[at, :] * (math.log2(math.e) / math.sqrt(q_ref.shape[1])))
                q_all = jnp.concatenate([high, low], axis=1)
                q_buf[at, :] = q_all
                row = lax.broadcasted_iota(jnp.int32, (CHUNK, 128), 0) + begin
                step(at, q_all, window, index * tokens + row // heads, base, k_buf, v_buf, lane_ref, qs_ref, acc_ref, m_ref, l_ref)

        fits = core * tokens + (tile + 1) * TILE <= short
        pl.when(fits)(lambda: attend((0, short)))
        pl.when(jnp.logical_not(fits))(lambda: attend((0, 2 * tokens)))
        return carry

    lax.fori_loop(0, rows // size, tile_body, 0)


def back_kernel(heads, units, trims, writer, info, low_ref, q_buf, qs_ref, acc_in, m_in, l_in, *rest):
    pieces, rest = rest[: 2 * len(units)], rest[2 * len(units) :]
    if writer == 0:
        _, out_hbm, k_buf, v_buf, lane_ref, out_ref, sems = rest
        acc_ref, m_ref, l_ref = acc_in, m_in, l_in
    elif writer == 1:
        acc_ref, m_ref, l_ref, out_hbm, k_buf, v_buf, lane_ref, out_ref, sems = rest
    else:
        acc_ref, m_ref, l_ref, k_buf, v_buf, lane_ref = rest
    index = info[0]
    rows = q_buf.shape[0]
    tokens = rows // heads
    size = TILE * heads
    core = index % 2
    writes = index // 2 % 2 == (-1 if writer is None else writer)
    fill_lanes(lane_ref)

    def out_copy(tile):
        at = pl.ds(pl.multiple_of(tile * size, size), size)
        return pltpu.make_async_copy(out_ref.at[at], out_hbm.at[at], sems.at[tile])

    def unit_body(n, carry):
        distance = jnp.int32(0)
        for m, pair in enumerate(units):
            distance = jnp.where(n == m, jnp.where(index // 2 % 2 == 0, pair[0], pair[1]), distance)
        base = (index - core - 2 * distance) * tokens
        end = jnp.where(distance > 0, base + 2 * tokens, -1)
        for m in range(len(units)):

            @pl.when((n == m) & (low_ref[0] < end))
            def _():
                place(pieces[2 * m], core * tokens, k_buf, v_buf)
                place(pieces[2 * m + 1], (1 - core) * tokens, k_buf, v_buf)

        def tile_body(tile, carry):
            skip = low_ref[tile] - base
            for begin, stop in zip(trims, trims[1:] + (2 * tokens,)):
                reached = (skip < stop) & (low_ref[tile] < end)
                if begin:
                    reached &= skip >= begin

                @pl.when(reached)
                def _():
                    for _, at in chunks(tile, size):
                        step(at, q_buf[at, :], (begin, 2 * tokens), None, base, k_buf, v_buf, lane_ref, qs_ref, acc_ref, m_ref, l_ref)

            if writer is not None:

                @pl.when(writes & (n == len(units) - 1))
                def _():
                    for _, at in chunks(tile, size):
                        out_ref[at, :] = acc_ref[at, :] / jnp.sum(l_ref[at, :], axis=1, keepdims=True)
                    out_copy(tile).start()

            return carry

        lax.fori_loop(0, rows // size, tile_body, 0)
        return carry

    if len(units) == 1:
        unit_body(0, 0)
    else:
        lax.fori_loop(0, len(units), unit_body, 0)
    if writer is not None:

        @pl.when(writes)
        def _():
            for tile in range(rows // size):
                out_copy(tile).wait()


VMEM = pl.BlockSpec(memory_space=pltpu.VMEM)
SMEM = pl.BlockSpec(memory_space=pltpu.SMEM)
HBM = pl.BlockSpec(memory_space=pltpu.HBM)
LIMIT = 24 << 20


def buffers(tokens):
    split = pltpu.VMEM((2 * tokens, 256), BF16)
    return [split, split, pltpu.VMEM((8, 2 * tokens), jnp.int32)]


def attend_own(heads, info, lens, q, mine, other):
    rows = q.shape[0]
    tokens = rows // heads
    full = jax.ShapeDtypeStruct((rows, 128), F32)
    return pl.pallas_call(
        functools.partial(own_kernel, heads),
        name="own_pair",
        out_shape=(
            full,
            full,
            full,
            jax.ShapeDtypeStruct((rows, 256), BF16),
            jax.ShapeDtypeStruct((rows, 128), jnp.int32),
            jax.ShapeDtypeStruct((rows // (TILE * heads),), jnp.int32),
        ),
        in_specs=[SMEM, HBM, HBM, VMEM, VMEM],
        out_specs=(VMEM, VMEM, VMEM, VMEM, VMEM, SMEM),
        scratch_shapes=buffers(tokens)
        + [pltpu.VMEM((rows, 128), F32), pltpu.VMEM(lens.shape, jnp.int32), pltpu.SemaphoreType.DMA((2,))],
        compiler_params=pltpu.CompilerParams(vmem_limit_bytes=LIMIT),
    )(info, lens, q, mine, other)


def attend_back(heads, units, trims, writer, info, low, q_buf, qs, state, pieces, out=None):
    rows = q_buf.shape[0]
    tokens = rows // heads
    full = jax.ShapeDtypeStruct((rows, 128), F32)
    tail = [pltpu.VMEM((rows, 128), F32), pltpu.SemaphoreType.DMA((rows // (TILE * heads),))]
    last = writer == 0
    results = 1 if last else 3 if writer is None else 4
    inputs = (info, low, q_buf, qs, *state, *pieces)
    return pl.pallas_call(
        functools.partial(back_kernel, heads, units, trims, writer),
        out_shape=full if last else (full,) * results,
        in_specs=[SMEM, SMEM] + [VMEM] * (5 + len(pieces)) + ([HBM] if last else []),
        out_specs=HBM if last else (VMEM, VMEM, VMEM, HBM)[:results],
        input_output_aliases={len(inputs): 0} if last else {4: 0, 5: 1, 6: 2},
        scratch_shapes=buffers(tokens) + ([] if writer is None else tail),
        compiler_params=pltpu.CompilerParams(vmem_limit_bytes=LIMIT),
    )(*inputs, *([out] if last else []))


def attend(queries, key_rows, value_rows, doc_lengths):
    tokens, heads, width = queries.shape
    count = lax.axis_size(AXES)
    index = lax.axis_index(AXES).astype(jnp.int32)
    info = jnp.reshape(index, (1,))
    q = pltpu.with_memory_space_constraint(queries.reshape(tokens * heads, width), pltpu.HBM)
    lens = pltpu.with_memory_space_constraint(doc_lengths.reshape(1, -1), pltpu.HBM)
    devices = range(count)
    even = [i for i in devices if i // 2 % 2 == 0]
    odd = [i for i in devices if i // 2 % 2 == 1]

    def send(x, pairs):
        return lax.ppermute(x, AXES, pairs)

    def swap(x, among=devices):
        return send(x, [(i, i ^ 1) for i in among])

    def after(x, state):
        x, *state = lax.optimization_barrier((x, *state))
        return x, state

    up = [(i, i + 4) for i in devices if i + 4 < count]
    held = jnp.stack([key_rows, value_rows]).reshape(2 * tokens, width)
    held_other = swap(held)
    up_1 = send(held, up)
    across_1 = send(held, [(i, i + 2) for i in even])
    *state, q_buf, qs, low = attend_own(heads, info, lens, q, held, held_other)

    def back(units, trims, writer, pieces, state, out=None):
        return attend_back(heads, units, trims, writer, info, low, q_buf, qs, state, pieces, out)

    up_1, state = after(up_1, state)
    up_2 = send(up_1, up)
    across_2 = send(up_1, [(i, i ^ 2) for i in devices])
    up_1_other = swap(up_1)
    across_1, state = after(across_1, state)
    across_1_other = swap(across_1, odd)
    state = back(((2, 2),), (0,), None, (up_1, up_1_other), state)
    up_2, state = after(up_2, state)
    across_3 = send(up_2, [(i, i - 2) for i in odd])
    up_2_other = swap(up_2)
    state = back(((0, 1),), (0,), None, (across_1, across_1_other), state)
    across_2, state = after(across_2, state)
    pieces = (up_2, up_2_other, across_2, swap(across_2))
    *state, out = back(((4, 4), (1, 3)), TRIMS, 1, pieces, state)
    across_3, state = after(across_3, state)
    out = back(((3, 0),), TRIMS, 0, (across_3, swap(across_3, even)), state, out)
    return out.reshape(tokens, heads, width)


def solution(mesh):
    in_specs = (P(AXES, None, None), P(AXES, None), P(AXES, None), P())
    return jax.shard_map(attend, mesh=mesh, in_specs=in_specs, out_specs=P(AXES, None, None), check_vma=False)
```
